128 devices in a mesh: row: 16 (over y, x_hi, core), col: 8 (over z, x_lo).
Axes of the slice: x: 4 (x_hi: 2, x_lo: 2; x = x_hi * 2 + x_lo), y: 4, z: 4, core: 2. Of those that a mesh axis runs over, the one named last changes fastest.
Arguments:
- features: float32 [8192, 256], P('row', 'col'), may hold values from -6 to 6
- weight: float32 [256, 256], replicated, may hold values from -0.375 to 0.375
- layer_bias: float32 [256], P('col'), may hold values from -3 to 3
- out_weight: float32 [2, 256], P(None, 'col'), may hold values from -0.375 to 0.375
- adj_tiles: float32 [16, 8, 4, 128, 128], P('row', 'col'), may hold values from -0.5 to 0.5
- tile_rows: int32 [16, 8, 4], P('row', 'col'), may hold values from 0 to 3
- tile_cols: int32 [16, 8, 4], P('row', 'col'), may hold values from 0 to 63, as said below
- tile_count: int32 [16, 8], P('row', 'col'), may hold values from 0 to 4, as said below
- port_rows: int32 [16, 128], P('row'), may hold values from 0 to 511
- targets: float32 [2, 2048], P(None, 'row'), may hold values from -6 to 6
Outputs:
- hidden: float32 [8192, 256], P('row', 'col')
- predictions: float32 [2, 2048], P(None, 'row')
- grad_weight: float32 [256, 256], P(None, 'col')
- grad_bias: float32 [256], P('col')
- grad_out_weight: float32 [2, 256], P(None, 'col')
The draws below stay inside these ranges and needn't reach their ends.
Inputs may be any that keep to these rules, and one draw needn't show every extreme that they name: tile_cols[r, c, k] >= 4 r + tile_rows[r, c, k]; the live slots of all devices name distinct tile positions. The live slots of a device are its first tile_count slots; some device has all 4 slots live.
All inputs are finite; a program needn't handle non-finite values.
Results may differ from the reference program's by a relative error of at most 0.00017.
Values sent between devices are 32-bit elements; how exact they have to be, the bound alone decides.
No kernel may reach another device: no remote copies, remote signals or barrier semaphores. Data moves between devices by JAX's collectives and lax.ppermute only.
A program may use at most 64 MiB of HBM per device.

```python
import jax
import jax.numpy as jnp
from jax import lax

FEAT = 256
TILE = 128
TR = 4
KT = 4
PORTS = 128
NODES = 8192
PORTS_ALL = 2048
N_ROW = 16
N_COL = 8


def tile_pattern(key):
    grid_tiles = N_ROW * TR
    candidates = TR * grid_tiles
    cand_index = jnp.arange(candidates, dtype=jnp.int32)
    local_row = cand_index // grid_tiles
    cand_col = cand_index % grid_tiles
    row_global = jnp.arange(N_ROW, dtype=jnp.int32)[:, None] * TR + local_row[None, :]
    distance = cand_col[None, :] - row_global
    usable = distance >= 0
    noise = jax.random.randint(jax.random.fold_in(key, 11), (N_ROW, candidates), 1, 65536, dtype=jnp.int32)
    score = jnp.where(usable, noise * (1 + jnp.maximum(distance, 0) // TR), jnp.int32(2097152))
    corner = (jnp.arange(N_ROW, dtype=jnp.int32)[:, None] == 0) & (cand_index[None, :] == grid_tiles - 1)
    score = jnp.where(corner, jnp.int32(0), score)
    combined = score * candidates + cand_index[None, :]
    order = jnp.argsort(combined, axis=1)[:, :N_COL * KT].astype(jnp.int32)
    rows_drawn = order // grid_tiles
    cols_drawn = order % grid_tiles
    usable_count = jnp.sum(usable.astype(jnp.int32), axis=1)
    slot_index = jnp.arange(N_COL * KT, dtype=jnp.int32)
    live = slot_index[None, :] < usable_count[:, None]
    cols_drawn = jnp.where(live, cols_drawn, grid_tiles - 1)
    rows_out = rows_drawn.reshape(N_ROW, KT, N_COL).transpose(0, 2, 1)
    cols_out = cols_drawn.reshape(N_ROW, KT, N_COL).transpose(0, 2, 1)
    live_out = live.astype(jnp.int32).reshape(N_ROW, KT, N_COL).transpose(0, 2, 1)
    struct_count = jnp.sum(live_out, axis=2).astype(jnp.int32)
    random_count = jax.random.randint(jax.random.fold_in(key, 23), (N_ROW, N_COL), 1, KT + 1, dtype=jnp.int32)
    first_device = (jnp.arange(N_ROW, dtype=jnp.int32)[:, None] == 0) & (jnp.arange(N_COL, dtype=jnp.int32)[None, :] == 0)
    random_count = jnp.where(first_device, jnp.int32(KT), random_count)
    count_out = jnp.minimum(struct_count, random_count).astype(jnp.int32)
    return (rows_out, cols_out, count_out)


def draw_tile_rows(key, part):
    return tile_pattern(key)[0]


def draw_tile_cols(key, part):
    return tile_pattern(key)[1]


def draw_tile_count(key, part):
    return tile_pattern(key)[2]


def set_ends(array, rng, low, top_value):
    index_at = [jax.random.randint(jax.random.fold_in(rng, axis), (), 0, length) for axis, length in enumerate(array.shape)]
    main_axis = array.shape.index(max(array.shape))
    beside = index_at[:main_axis] + [(index_at[main_axis] + 1) % array.shape[main_axis]] + index_at[main_axis + 1:]
    return array.at[tuple(index_at)].set(low).at[tuple(beside)].set(top_value)


def shard_levels(key, shape, split, least, largest):
    def one(dim, blocks):
        steps = jax.random.uniform(jax.random.fold_in(jax.random.fold_in(key, 6), dim), (blocks,), jnp.float32, least / len(split), largest / len(split))
        return jnp.repeat(jnp.exp(steps), shape[dim] // blocks).reshape((-1,) + (1,) * (len(shape) - dim - 1))

    level = one(*split[0])
    for cut in split[1:]:
        level = level * one(*cut)
    return level


def scatter_about(rng, dims, deviation, most, cuts=(), held_as=jnp.bfloat16):
    drawn = deviation * jax.random.normal(rng, dims, jnp.float32)
    if cuts:
        drawn = drawn * shard_levels(rng, dims, cuts, -0.22, 0.18)
    return jnp.clip(drawn, -most, most).astype(held_as)


def setup_inputs(seed: int = 0) -> dict:
    key_of = jax.random.split(jax.random.key(seed), 11)
    return {
        "features": scatter_about(key_of[0], (NODES, FEAT), 1.0, 6.0, ((0, 16), (1, 8)), jnp.float32),
        "weight": scatter_about(key_of[1], (FEAT, FEAT), FEAT ** -0.5, 0.375, (), jnp.float32),
        "layer_bias": scatter_about(key_of[2], (FEAT,), 0.5, 3.0, ((0, 8),), jnp.float32),
        "out_weight": scatter_about(key_of[3], (2, FEAT), FEAT ** -0.5, 0.375, ((1, 8),), jnp.float32),
        "adj_tiles": scatter_about(key_of[4], (N_ROW, N_COL, KT, TILE, TILE), ((128 * N_COL * KT // TR) ** -0.5), 0.5, ((0, 16), (1, 8)), jnp.float32),
        "tile_rows": draw_tile_rows(jax.random.fold_in(key_of[10], 71), 0),
        "tile_cols": draw_tile_cols(jax.random.fold_in(key_of[10], 71), 0),
        "tile_count": draw_tile_count(jax.random.fold_in(key_of[10], 71), 0),
        "port_rows": set_ends(jax.random.randint(key_of[8], (N_ROW, PORTS), 0, TR * TILE), jax.random.fold_in(key_of[8], 1), 0, (TR * TILE) - 1).astype(jnp.int32),
        "targets": scatter_about(key_of[9], (2, PORTS_ALL), 1.0, 6.0, ((1, 16),), jnp.float32),
    }


def aggregate(field, adj_tiles, tile_rows, tile_cols, tile_count):
    feat_width = field.shape[1]
    slot_total = tile_rows.shape[2]
    row_global = (jnp.arange(N_ROW, dtype=jnp.int32)[:, None, None] * TR + tile_rows).reshape(-1, slot_total)
    col_global = tile_cols.reshape(-1, slot_total)
    live_mask = (jnp.arange(slot_total, dtype=jnp.int32)[None, None, :] < tile_count[:, :, None]).astype(jnp.float32).reshape(-1, slot_total)
    tile_data = adj_tiles.reshape(-1, slot_total, TILE, TILE)
    blocks = field.reshape(N_ROW * TR, TILE, feat_width)

    def add_device(totals, device_item):
        tile_block, row_index, col_index, mask_row = device_item
        masked = tile_block * mask_row[:, None, None]
        direct = jnp.einsum("kab,kbf->kaf", masked, blocks[col_index], precision=lax.Precision.HIGHEST)
        mirror = jnp.einsum("kab,kaf->kbf", masked, blocks[row_index], precision=lax.Precision.HIGHEST)
        totals = totals.at[row_index].add(direct).at[col_index].add(mirror)
        return totals, None

    start = jnp.zeros((N_ROW * TR, TILE, feat_width), jnp.float32)
    totals, unused = lax.scan(add_device, start, (tile_data, row_global, col_global, live_mask))
    return totals.reshape(-1, feat_width)


def reference(features, weight, layer_bias, out_weight, adj_tiles, tile_rows, tile_cols, tile_count, port_rows, targets):
    z_rows = jnp.dot(features, weight, precision=lax.Precision.HIGHEST)
    pre = aggregate(z_rows, adj_tiles, tile_rows, tile_cols, tile_count) + layer_bias[None, :]
    sigma = jax.nn.sigmoid(pre)
    hidden = pre * sigma
    port_global = (jnp.arange(N_ROW, dtype=jnp.int32)[:, None] * (TR * TILE) + port_rows).reshape(-1)
    port_hidden = hidden[port_global]
    predictions = jnp.dot(out_weight, port_hidden.T, precision=lax.Precision.HIGHEST)
    errors = predictions - targets
    grad_out_weight = jnp.dot(errors, port_hidden, precision=lax.Precision.HIGHEST)
    port_grad = jnp.dot(errors.T, out_weight, precision=lax.Precision.HIGHEST)
    grad_hidden = jnp.zeros_like(hidden).at[port_global].add(port_grad)
    grad_pre = grad_hidden * (sigma * (1.0 + pre * (1.0 - sigma)))
    back = aggregate(grad_pre, adj_tiles, tile_rows, tile_cols, tile_count)
    grad_weight = jnp.dot(features.T, back, precision=lax.Precision.HIGHEST)
    grad_bias = jnp.sum(grad_pre, axis=0)
    return (hidden, predictions, grad_weight, grad_bias, grad_out_weight)
```

```python
import functools

import jax
import jax.numpy as jnp
from jax import lax
from jax.experimental import pallas as pl
from jax.experimental.pallas import tpu as pltpu
from jax.sharding import PartitionSpec as P

F32 = jnp.float32
BF16 = jnp.bfloat16
VMEM = pl.BlockSpec(memory_space=pltpu.VMEM)
SMEM = pl.BlockSpec(memory_space=pltpu.SMEM)
NN = (((1,), (0,)), ((), ()))
NT = (((1,), (1,)), ((), ()))
TN = (((0,), (0,)), ((), ()))


def split(x):
    high = x.astype(BF16)
    low = (x - high.astype(F32)).astype(BF16)
    return high, low


def dot3(a, b, dims):
    ah, al = a
    bh, bl = b
    one = functools.partial(lax.dot_general, dimension_numbers=dims, preferred_element_type=F32)
    return one(ah, bh) + (one(al, bh) + one(ah, bl))


def stacked_dot3(a, b, dims):
    rows = a[0].shape[0]
    one = functools.partial(lax.dot_general, dimension_numbers=dims, preferred_element_type=F32)
    both = one(jnp.concatenate(a, axis=0), b[0])
    return both[:rows] + (both[rows:] + one(a[0], b[1]))


def pack_kernel(slots, rows_ref, cols_ref, count_ref, tiles_ref, side_ref, out_ref):
    edge = tiles_ref.shape[3]
    for k in range(slots):
        live = k < count_ref[0, 0]
        out_ref[0, k * edge : (k + 1) * edge, :] = jnp.where(live, tiles_ref[0, 0, k], 0.0)
    lane = lax.broadcasted_iota(jnp.int32, (1, edge), 1)
    meta = jnp.zeros((1, edge), jnp.int32)
    for k in range(slots):
        meta = jnp.where(lane == k, rows_ref[0, 0, k], meta)
        meta = jnp.where(lane == slots + k, cols_ref[0, 0, k], meta)
    out_ref[0, slots * edge : slots * edge + 8, :] = side_ref[...]
    out_ref[0, slots * edge : slots * edge + 1, :] = meta.astype(F32)


def mirror_kernel(slots, meta_ref, tiles_ref, x_ref, out_ref):
    edge = tiles_ref.shape[2]
    row_tiles = x_ref.shape[1] // edge
    out_ref[...] = jnp.zeros_like(out_ref)
    for d in range(tiles_ref.shape[0]):
        for k in range(slots):
            row = meta_ref[d, k]
            col = meta_ref[d, slots + k]
            x = split(x_ref[:, pl.ds(pl.multiple_of(row * edge, edge), edge)])
            u = split(tiles_ref[d, k * edge : (k + 1) * edge, :])
            lanes = pl.ds(pl.multiple_of((col % row_tiles) * edge, edge), edge)
            out_ref[col // row_tiles, :, lanes] += stacked_dot3(x, u, NN)


def direct_kernel(slots, meta_ref, tiles_ref, x_ref, part_ref, out_ref, total):
    edge = tiles_ref.shape[2]
    row_tiles = total.shape[1] // edge
    total[...] = jnp.sum(part_ref[...], axis=0)
    for d in range(tiles_ref.shape[0]):
        for k in range(slots):
            row = meta_ref[d, k]
            col = meta_ref[d, slots + k]
            lanes = pl.ds(pl.multiple_of((col % row_tiles) * edge, edge), edge)
            x = split(x_ref[col // row_tiles, :, lanes])
            u = split(tiles_ref[d, k * edge : (k + 1) * edge, :])
            here = pl.ds(pl.multiple_of(row * edge, edge), edge)
            total[:, here] += stacked_dot3(x, u, NT)
    for c in range(out_ref.shape[0]):
        out_ref[c] = total[...]


def main_kernel(
    y_ref, w_ref, side_ref, ports_ref, targets_ref, hidden_ref, pred_ref, grad_ref, wt, pre_p, hid_p, side_t
):
    me = lax.axis_index("col")
    cols, block, nodes = y_ref.shape
    feats = cols * block
    mine = pl.ds(pl.multiple_of(me * block, block), block)
    wt[...] = w_ref[...].T
    y = split(y_ref[...].reshape(feats, nodes))
    for c in range(cols):
        side_t[c * block : (c + 1) * block, :] = side_ref[c].T[:block, :]
    pre = stacked_dot3(split(wt[mine, :]), y, NN) + side_t[mine, 1:2]
    hidden_ref[...] = pre * jax.nn.sigmoid(pre)
    node = lax.broadcasted_iota(jnp.int32, (nodes, ports_ref.shape[1]), 0)
    pick = (node == ports_ref[...]).astype(BF16)
    one = functools.partial(lax.dot_general, dimension_numbers=NN, preferred_element_type=F32)
    yp = split(one(y[0], pick) + one(y[1], pick))
    pre_all = dot3(split(wt[...]), yp, NN) + side_t[:, 1:2]
    pre_p[...] = pre_all
    hid_all = pre_all * jax.nn.sigmoid(pre_all)
    hid_p[...] = hid_all
    weights = jnp.concatenate([side_ref[c, 2:4, :block] for c in range(cols)], axis=1)
    pred = dot3(split(weights), split(hid_all), NN)
    pred_ref[...] = pred
    err = pred - targets_ref[...]
    gow = dot3(split(err), split(hid_p[mine, :]), NT)
    pre_c = pre_p[mine, :]
    s = jax.nn.sigmoid(pre_c)
    port_grad = side_t[mine, 2:3] * err[0:1, :] + side_t[mine, 3:4] * err[1:2, :]
    grad_pre = port_grad * (s * (1.0 + pre_c * (1.0 - s)))
    gp = split(grad_pre)
    gw = stacked_dot3(gp, yp, NT)
    ones = jnp.ones((1, grad_pre.shape[1]), BF16)
    gb = lax.dot_general(ones, gp[0], NT, preferred_element_type=F32) + lax.dot_general(
        ones, gp[1], NT, preferred_element_type=F32
    )
    for r in range(grad_ref.shape[0]):
        grad_ref[r, :block, :] = gw
        grad_ref[r, block : block + 2, :block] = gow
        grad_ref[r, block + 2 : block + 3, :block] = gb


def final_kernel(parts_ref, gw_ref, gb_ref, gow_ref):
    block = gw_ref.shape[0]
    total = jnp.sum(parts_ref[...], axis=0)
    gw_ref[...] = total[:block, :]
    gow_ref[...] = total[block : block + 2, :block]
    gb_ref[...] = total[block + 2 : block + 3, :block]


def per_device(
    features,
    weight,
    layer_bias,
    out_weight,
    adj_tiles,
    tile_rows,
    tile_cols,
    tile_count,
    port_rows,
    targets,
):
    rows = lax.axis_size("row")
    cols = lax.axis_size("col")
    nodes, block = features.shape
    feats = weight.shape[0]
    slots, edge = adj_tiles.shape[2:4]
    outs = out_weight.shape[0]
    x_own = features.T
    x_all = lax.all_gather(x_own, "row", axis=0)

    side = jnp.zeros((8, edge), F32)
    side = side.at[1, :block].set(layer_bias).at[2 : 2 + outs, :block].set(out_weight)
    length = slots * edge + 8
    packed = pl.pallas_call(
        functools.partial(pack_kernel, slots),
        grid=(cols,),
        in_specs=[
            SMEM,
            SMEM,
            SMEM,
            pl.BlockSpec((1, 1, slots, edge, edge), lambda i: (0, 0, 0, 0, 0)),
            pl.BlockSpec((8, edge), lambda i: (0, 0)),
        ],
        out_specs=pl.BlockSpec((1, length, edge), lambda i: (i, 0, 0)),
        out_shape=jax.ShapeDtypeStruct((cols, length, edge), F32),
        name="pack",
    )(tile_rows, tile_cols, tile_count, adj_tiles, side)
    tiles = lax.all_to_all(packed, "col", 0, 0)
    meta = tiles[:, slots * edge, : 2 * slots].astype(jnp.int32)
    sides = tiles[:, slots * edge :, :]

    mirror = pl.pallas_call(
        functools.partial(mirror_kernel, slots),
        in_specs=[SMEM, VMEM, VMEM],
        out_specs=VMEM,
        out_shape=jax.ShapeDtypeStruct((rows, block, nodes), F32),
        name="mirror",
    )(meta, tiles, x_own)
    parts = lax.all_to_all(mirror, "row", 0, 0)
    y_own = pl.pallas_call(
        functools.partial(direct_kernel, slots),
        in_specs=[SMEM, VMEM, VMEM, VMEM],
        out_specs=VMEM,
        out_shape=jax.ShapeDtypeStruct((cols, block, nodes), F32),
        scratch_shapes=[pltpu.VMEM((block, nodes), F32)],
        name="direct",
    )(meta, tiles, x_all, parts)
    y = lax.all_to_all(y_own, "col", 0, 0)
    ports = port_rows.shape[1]
    hidden_t, predictions, grads = pl.pallas_call(
        main_kernel,
        in_specs=[VMEM] * 5,
        out_specs=[VMEM] * 3,
        out_shape=[
            jax.ShapeDtypeStruct((block, nodes), F32),
            jax.ShapeDtypeStruct((outs, ports), F32),
            jax.ShapeDtypeStruct((rows, block + 8, feats), F32),
        ],
        scratch_shapes=[
            pltpu.VMEM((feats, feats), F32),
            pltpu.VMEM((feats, ports), F32),
            pltpu.VMEM((feats, ports), F32),
            pltpu.VMEM((feats, 8), F32),
        ],
        name="main",
    )(y, weight, sides, port_rows, targets)
    all_grads = lax.all_to_all(grads, "row", 0, 0)
    gw, gb, gow = pl.pallas_call(
        final_kernel,
        in_specs=[VMEM],
        out_specs=[VMEM] * 3,
        out_shape=[
            jax.ShapeDtypeStruct((block, feats), F32),
            jax.ShapeDtypeStruct((1, block), F32),
            jax.ShapeDtypeStruct((outs, block), F32),
        ],
        name="final",
    )(all_grads)
    return (hidden_t.T, predictions, gw.T, gb[0], gow)


def solution(mesh):
    placed = (
        P("row", "col"),
        P(),
        P("col"),
        P(None, "col"),
        P("row", "col", None, None, None),
        P("row", "col", None),
        P("row", "col", None),
        P("row", "col"),
        P("row", None),
        P(None, "row"),
    )
    return jax.shard_map(
        per_device,
        mesh=mesh,
        in_specs=placed,
        out_specs=(P("row", "col"), P(None, "row"), P(None, "col"), P("col"), P(None, "col")),
        check_vma=False,
    )
```

```python
import functools

import jax
import jax.numpy as jnp
from jax import lax
from jax.experimental import pallas as pl
from jax.experimental.pallas import tpu as pltpu
from jax.sharding import PartitionSpec as P

F32 = jnp.float32
BF16 = jnp.bfloat16
VMEM = pl.BlockSpec(memory_space=pltpu.VMEM)
SMEM = pl.BlockSpec(memory_space=pltpu.SMEM)
NN = (((1,), (0,)), ((), ()))
NT = (((1,), (1,)), ((), ()))


def split(x):
    high = x.astype(BF16)
    low = (x - high.astype(F32)).astype(BF16)
    return high, low


def dot(a, b, dims):
    return lax.dot_general(a, b, dims, preferred_element_type=F32)


def dot3(a, b, dims):
    return dot(a[0], b[0], dims) + (dot(a[1], b[0], dims) + dot(a[0], b[1], dims))


def tile_dot(x, u, dims):
    rows = x[0].shape[0]
    wide = 1 if dims == NN else 0
    edge = u[0].shape[wide]
    every = dot(jnp.concatenate(x, axis=0), jnp.concatenate(u, axis=wide), dims)
    return every[:rows, :edge] + (every[rows:, :edge] + every[:rows, edge:] + every[rows:, edge:])


def pack_kernel(slots, rows_ref, cols_ref, count_ref, tiles_ref, bias_ref, readout_ref, out_ref, buf, sems):
    edge = tiles_ref.shape[2]
    block = bias_ref.shape[1]
    outs = readout_ref.shape[0]
    base = slots * edge
    copies = []
    for c in range(out_ref.shape[0]):
        here = out_ref.at[c, pl.ds(0, base), :]
        copies.append(pltpu.make_async_copy(tiles_ref.at[0], here, sems.at[0, c]))
        copies[-1].start()
    lane = lax.broadcasted_iota(jnp.int32, (1, edge), 1)
    meta = jnp.where(lane == 2 * slots, count_ref[0, 0], 0)
    for k in range(slots):
        meta = jnp.where(lane == k, rows_ref[0, 0, k], meta)
        meta = jnp.where(lane == slots + k, cols_ref[0, 0, k], meta)
    buf[...] = jnp.zeros(buf.shape, F32)
    buf[0:1, :] = meta.astype(F32)
    buf[1:2, :block] = bias_ref[...]
    buf[2 : 2 + outs, :block] = readout_ref[...]
    for c in range(out_ref.shape[0]):
        copies.append(pltpu.make_async_copy(buf, out_ref.at[c, pl.ds(base, 8), :], sems.at[1, c]))
        copies[-1].start()
    for copy in copies:
        copy.wait()


def read_meta(slots, tiles_ref, meta, sem):
    edge = tiles_ref.shape[2]
    copy = pltpu.make_async_copy(tiles_ref.at[:, pl.ds(slots * edge, 8), :], meta, sem)
    copy.start()
    return copy


def slot_of(slots, meta, d, k):
    row, col, count = [meta[d, 0, at].astype(jnp.int32) for at in (k, slots + k, 2 * slots)]
    return row, col, k < count


def mirror_kernel(slots, tiles_ref, x_ref, keep_ref, send_ref, side_ref, copy_ref, total, meta, sem, copy_sem):
    edge = tiles_ref.shape[2]
    row_tiles = x_ref.shape[1] // edge
    core = lax.axis_index("row") % 2
    copy = read_meta(slots, tiles_ref, meta, sem)
    spare = pltpu.make_async_copy(tiles_ref, copy_ref, copy_sem)
    spare.start()
    total[...] = jnp.zeros_like(total)
    side_ref[...] = tiles_ref[:, slots * edge :, :]
    copy.wait()
    for d in range(tiles_ref.shape[0]):
        for k in range(slots):
            row, col, live = slot_of(slots, meta, d, k)
            x = x_ref[:, pl.ds(pl.multiple_of(row * edge, edge), edge)]
            x = split(jnp.where(live, x, 0.0))
            u = split(tiles_ref[d, k * edge : (k + 1) * edge, :])
            lanes = pl.ds(pl.multiple_of((col % row_tiles) * edge, edge), edge)
            piece = col // row_tiles
            total[(piece % 2) ^ core, piece // 2, :, lanes] += tile_dot(x, u, NN)
    keep_ref[...] = total[0]
    send_ref[...] = total[1]
    spare.wait()


def add_kernel(a_ref, b_ref, out_ref):
    total = a_ref[...] + b_ref[...]
    if out_ref.shape == a_ref.shape:
        out_ref[...] = total
    else:
        for p in range(out_ref.shape[0]):
            out_ref[p] = total


def xor_steps(rows):
    return [2, 4, 8, 1] if rows == 16 else [1 << i for i in range(rows.bit_length() - 2, -1, -1)]


def xor_slots(rows):
    pieces = [[0]]
    for bit in xor_steps(rows):
        pieces.append([mask ^ bit for piece in pieces for mask in piece])
    return pieces


def xor_exchange(x, bit, rows):
    return lax.ppermute(x, "row", [(i, i ^ bit) for i in range(rows)])


def direct_kernel(slots, *refs):
    tiles_ref, pieces, out_ref, x_all, meta, sem = refs[0], refs[1:-4], refs[-4], refs[-3], refs[-2], refs[-1]
    me = lax.axis_index("row")
    edge = tiles_ref.shape[2]
    row_tiles = out_ref.shape[1] // edge
    copy = read_meta(slots, tiles_ref, meta, sem)
    out_ref[...] = jnp.zeros_like(out_ref)
    for piece, slots_of in zip(pieces, xor_slots(x_all.shape[0])):
        for at, slot in enumerate(slots_of):
            x_all[slot] = piece[at]
    copy.wait()
    for d in range(tiles_ref.shape[0]):
        for k in range(slots):
            row, col, live = slot_of(slots, meta, d, k)
            lanes = pl.ds(pl.multiple_of((col % row_tiles) * edge, edge), edge)
            x = split(jnp.where(live, x_all[(col // row_tiles) ^ me, :, lanes], 0.0))
            u = split(tiles_ref[d, k * edge : (k + 1) * edge, :])
            here = pl.ds(pl.multiple_of(row * edge, edge), edge)
            out_ref[:, here] += tile_dot(x, u, NT)


def gather_sum_kernel(part_ref, direct_ref, out_ref):
    total = direct_ref[...]
    for r in range(part_ref.shape[0]):
        total = total + part_ref[r]
    for c in range(out_ref.shape[0]):
        out_ref[c] = total


def prep_kernel(w_ref, side_ref, wt_ref, side_t_ref, readout_ref):
    wt = split(w_ref[...].T)
    wt_ref[0] = wt[0]
    wt_ref[1] = wt[1]
    cols = side_ref.shape[0]
    block = w_ref.shape[0] // cols
    for c in range(cols):
        side = side_ref[c]
        side_t_ref[c * block : (c + 1) * block, :] = side.T[:block, :]
        readout_ref[:, c * block : (c + 1) * block] = side[:, :block]


def ports_kernel(
    y_ref, wt_ref, side_t_ref, readout_ref, ports_ref, targets_ref, pred_ref, grad_ref, pre_p, hid_p
):
    me = lax.axis_index("col")
    cols, block, nodes = y_ref.shape
    feats = cols * block
    mine = pl.ds(pl.multiple_of(me * block, block), block)
    y = split(y_ref[...].reshape(feats, nodes))
    node = lax.broadcasted_iota(jnp.int32, (nodes, ports_ref.shape[1]), 0)
    pick = (node == ports_ref[...]).astype(BF16)
    yp = split(dot(y[0], pick, NN) + dot(y[1], pick, NN))
    pre_all = dot3((wt_ref[0], wt_ref[1]), yp, NN) + side_t_ref[:, 1:2]
    pre_p[...] = pre_all
    hid_all = pre_all * jax.nn.sigmoid(pre_all)
    hid_p[...] = hid_all
    outs = targets_ref.shape[0]
    pred = dot3(split(readout_ref[...]), split(hid_all), NN)[2 : 2 + outs]
    pred_ref[...] = pred
    err = pred - targets_ref[...]
    gow = dot3(split(err), split(hid_p[mine, :]), NT)
    pre_c = pre_p[mine, :]
    s = jax.nn.sigmoid(pre_c)
    port_grad = side_t_ref[mine, 2:3] * err[0:1, :] + side_t_ref[mine, 3:4] * err[1:2, :]
    grad_pre = port_grad * (s * (1.0 + pre_c * (1.0 - s)))
    gp = split(grad_pre)
    ones = jnp.ones((1, grad_pre.shape[1]), BF16)
    gb = dot(ones, gp[0], NT) + dot(ones, gp[1], NT)
    gw = dot3(gp, yp, NT)
    grad_ref[:block, :] = gw
    grad_ref[block:, :] = jnp.zeros((grad_ref.shape[0] - block, feats), F32)
    grad_ref[block : block + outs, :block] = gow
    grad_ref[block + outs : block + outs + 1, :block] = gb


def hidden_kernel(y_ref, wt_ref, side_t_ref, hidden_ref):
    me = lax.axis_index("col")
    cols, block, nodes = y_ref.shape
    mine = pl.ds(pl.multiple_of(me * block, block), block)
    y = split(y_ref[...].reshape(cols * block, nodes))
    pre = dot3((wt_ref[0, mine, :], wt_ref[1, mine, :]), y, NN) + side_t_ref[mine, 1:2]
    hidden_ref[...] = pre * jax.nn.sigmoid(pre)


def final_kernel(parts_ref, gw_ref, gb_ref, gow_ref):
    block = gw_ref.shape[0]
    outs = gow_ref.shape[0]
    total = parts_ref[0]
    for r in range(1, parts_ref.shape[0]):
        total = total + parts_ref[r]
    gw_ref[...] = total[:block, :]
    gow_ref[...] = total[block : block + outs, :block]
    gb_ref[...] = total[block + outs : block + outs + 1, :block]


def on_chip(x):
    return pltpu.with_memory_space_constraint(x, pltpu.VMEM)


def per_device(
    features,
    weight,
    layer_bias,
    out_weight,
    adj_tiles,
    tile_rows,
    tile_cols,
    tile_count,
    port_rows,
    targets,
):
    rows = lax.axis_size("row")
    cols = lax.axis_size("col")
    nodes, block = features.shape
    feats = weight.shape[0]
    slots, edge = adj_tiles.shape[2:4]
    outs = out_weight.shape[0]
    x_own = features.T
    base = slots * edge
    length = base + 8

    anywhere = pl.BlockSpec(memory_space=pl.ANY)
    packed = pl.pallas_call(
        functools.partial(pack_kernel, slots),
        in_specs=[SMEM, SMEM, SMEM, VMEM, VMEM, VMEM],
        out_specs=anywhere,
        out_shape=jax.ShapeDtypeStruct((cols, length, edge), F32),
        scratch_shapes=[pltpu.VMEM((8, edge), F32), pltpu.SemaphoreType.DMA((2, cols))],
        name="pack",
    )(tile_rows, tile_cols, tile_count, adj_tiles.reshape(1, base, edge), layer_bias[None, :], out_weight)
    steps = xor_steps(rows)
    first = xor_exchange(x_own[None], steps[0], rows)
    packed, first = lax.optimization_barrier((packed, first))
    tiles = on_chip(lax.all_to_all(packed, "col", 0, 0))
    pieces = [x_own[None], first]
    for bit in steps[1:]:
        pieces.append(xor_exchange(jnp.concatenate(pieces, axis=0), bit, rows))
    x_first, pieces[-1] = lax.optimization_barrier((x_own, pieces[-1]))

    meta = [pltpu.SMEM((cols, 8, edge), F32), pltpu.SemaphoreType.DMA]
    half = (rows // 2, block, nodes)
    keep, send, sides, spare_tiles = pl.pallas_call(
        functools.partial(mirror_kernel, slots),
        in_specs=[VMEM, VMEM],
        out_specs=[VMEM] * 3 + [anywhere],
        out_shape=[
            pltpu.VMEM(half, F32),
            pltpu.VMEM(half, F32),
            pltpu.VMEM((cols, 8, edge), F32),
            jax.ShapeDtypeStruct((cols, length, edge), F32),
        ],
        scratch_shapes=[pltpu.VMEM((2,) + half, F32)] + meta + [pltpu.SemaphoreType.DMA],
        name="mirror",
    )(tiles, x_first)
    other_core = [(r, r ^ 1) for r in range(rows)]
    chips = [list(range(core, rows, 2)) for core in range(2)]
    paired = pl.pallas_call(
        add_kernel,
        in_specs=[VMEM, VMEM],
        out_specs=VMEM,
        out_shape=pltpu.VMEM(half, F32),
        name="pair_sum",
    )(on_chip(keep), on_chip(lax.ppermute(send, "row", other_core)))
    parts = on_chip(lax.all_to_all(paired, "row", 0, 0, axis_index_groups=chips))
    direct = pl.pallas_call(
        functools.partial(direct_kernel, slots),
        in_specs=[VMEM] * (1 + len(pieces)),
        out_specs=VMEM,
        out_shape=pltpu.VMEM((block, nodes), F32),
        scratch_shapes=[pltpu.VMEM((rows, block, nodes), F32)] + meta,
        name="direct",
    )(spare_tiles, *pieces)
    wt, side_t, readout = pl.pallas_call(
        prep_kernel,
        in_specs=[VMEM] * 2,
        out_specs=[VMEM] * 3,
        out_shape=[
            pltpu.VMEM((2, feats, feats), BF16),
            pltpu.VMEM((feats, 8), F32),
            pltpu.VMEM((8, feats), F32),
        ],
        name="prep",
    )(weight, on_chip(sides))
    wt, side_t, readout = on_chip(wt), on_chip(side_t), on_chip(readout)
    y_own = pl.pallas_call(
        gather_sum_kernel,
        in_specs=[VMEM, VMEM],
        out_specs=VMEM,
        out_shape=pltpu.VMEM((cols, block, nodes), F32),
        name="gather_sum",
    )(parts, on_chip(direct))
    y = on_chip(lax.all_to_all(y_own, "col", 0, 0))
    ports = port_rows.shape[1]
    predictions, grads = pl.pallas_call(
        ports_kernel,
        in_specs=[VMEM] * 6,
        out_specs=[VMEM, VMEM],
        out_shape=[
            jax.ShapeDtypeStruct((outs, ports), F32),
            pltpu.VMEM((block + 8, feats), F32),
        ],
        scratch_shapes=[pltpu.VMEM((feats, ports), F32)] * 2,
        name="ports",
    )(y, wt, side_t, readout, port_rows, targets)
    pair_grads = pl.pallas_call(
        add_kernel,
        in_specs=[VMEM, VMEM],
        out_specs=VMEM,
        out_shape=pltpu.VMEM((rows // 2, block + 8, feats), F32),
        name="pair_grads",
    )(on_chip(grads), on_chip(lax.ppermute(grads, "row", other_core)))
    all_grads = on_chip(lax.all_to_all(pair_grads, "row", 0, 0, axis_index_groups=chips))
    hidden_t = pl.pallas_call(
        hidden_kernel,
        in_specs=[VMEM] * 3,
        out_specs=VMEM,
        out_shape=jax.ShapeDtypeStruct((block, nodes), F32),
        name="hidden",
    )(y, wt, side_t)
    gw, gb, gow = pl.pallas_call(
        final_kernel,
        in_specs=[VMEM],
        out_specs=[VMEM] * 3,
        out_shape=[
            jax.ShapeDtypeStruct((block, feats), F32),
            jax.ShapeDtypeStruct((1, block), F32),
            jax.ShapeDtypeStruct((outs, block), F32),
        ],
        name="final",
    )(all_grads)
    return (hidden_t.T, predictions, gw.T, gb[0], gow)


def solution(mesh):
    placed = (
        P("row", "col"),
        P(),
        P("col"),
        P(None, "col"),
        P("row", "col", None, None, None),
        P("row", "col", None),
        P("row", "col", None),
        P("row", "col"),
        P("row", None),
        P(None, "row"),
    )
    return jax.shard_map(
        per_device,
        mesh=mesh,
        in_specs=placed,
        out_specs=(P("row", "col"), P(None, "row"), P(None, "col"), P("col"), P(None, "col")),
        check_vma=False,
    )
```

```python
import functools

import jax
import jax.numpy as jnp
from jax import lax
from jax.experimental import pallas as pl
from jax.experimental.pallas import tpu as pltpu
from jax.sharding import PartitionSpec as P

F32 = jnp.float32
BF16 = jnp.bfloat16
VMEM = pl.BlockSpec(memory_space=pltpu.VMEM)
SMEM = pl.BlockSpec(memory_space=pltpu.SMEM)
NN = (((1,), (0,)), ((), ()))
NT = (((1,), (1,)), ((), ()))
TILE_ORDER = [5, 1, 7, 3, 4, 2, 6]


def split(x):
    high = x.astype(BF16)
    low = (x - high.astype(F32)).astype(BF16)
    return high, low


def dot(a, b, dims):
    return lax.dot_general(a, b, dims, preferred_element_type=F32)


def dot3(a, b, dims):
    return dot(a[0], b[0], dims) + (dot(a[1], b[0], dims) + dot(a[0], b[1], dims))


def tile_dot(x, u, dims):
    rows = x[0].shape[0]
    wide = 1 if dims == NN else 0
    edge = u[0].shape[wide]
    every = dot(jnp.concatenate(x, axis=0), jnp.concatenate(u, axis=wide), dims)
    return every[:rows, :edge] + (every[rows:, :edge] + every[:rows, edge:] + every[rows:, edge:])


def pack_kernel(slots, rows_ref, cols_ref, count_ref, tiles_ref, bias_ref, readout_ref, out_ref, own_ref):
    edge = tiles_ref.shape[2]
    block = bias_ref.shape[1]
    outs = readout_ref.shape[0]
    base = slots * edge
    out_ref[:base, :] = tiles_ref[0]
    lane = lax.broadcasted_iota(jnp.int32, (1, edge), 1)
    meta = jnp.where(lane == 2 * slots, count_ref[0, 0], 0)
    for k in range(slots):
        meta = jnp.where(lane == k, rows_ref[0, 0, k], meta)
        meta = jnp.where(lane == slots + k, cols_ref[0, 0, k], meta)
    out_ref[base : base + 8, :] = jnp.zeros((8, edge), F32)
    out_ref[base : base + 1, :] = meta.astype(F32)
    out_ref[base + 1 : base + 2, :block] = bias_ref[...]
    out_ref[base + 2 : base + 2 + outs, :block] = readout_ref[...]
    own_ref[...] = out_ref[...]


def start_all(pairs, sems):
    copies = [pltpu.make_async_copy(src, dst, sems.at[i]) for i, (src, dst) in enumerate(pairs)]
    for copy in copies:
        copy.start()
    return copies


def slot_of(slots, meta, d, k):
    row, col, count = [meta[d, 0, at].astype(jnp.int32) for at in (k, slots + k, 2 * slots)]
    return row, col, k < count


def mirror_kernel(slots, order, *refs):
    tiles_refs, refs = refs[: len(order)], refs[len(order) :]
    x_ref, keep_ref, send_ref, side_ref, copy_ref, total, meta, meta_sems, copy_sems = refs
    edge = tiles_refs[0].shape[1]
    base = slots * edge
    row_tiles = x_ref.shape[1] // edge
    core = lax.axis_index("row") % 2
    metas = start_all([(ref.at[pl.ds(base, 8), :], meta.at[d]) for d, ref in enumerate(tiles_refs)], meta_sems)
    spares = start_all([(ref, copy_ref.at[d]) for d, ref in enumerate(tiles_refs)], copy_sems)
    total[...] = jnp.zeros_like(total)
    for d, ref in enumerate(tiles_refs):
        side_ref[d] = ref[base:, :]
    for d, ref in enumerate(tiles_refs):
        metas[d].wait()
        for k in range(slots):
            row, col, live = slot_of(slots, meta, d, k)
            x = x_ref[:, pl.ds(pl.multiple_of(row * edge, edge), edge)]
            x = split(jnp.where(live, x, 0.0))
            u = split(ref[k * edge : (k + 1) * edge, :])
            lanes = pl.ds(pl.multiple_of((col % row_tiles) * edge, edge), edge)
            piece = col // row_tiles
            total[(piece % 2) ^ core, piece // 2, :, lanes] += tile_dot(x, u, NN)
    keep_ref[...] = total[0]
    send_ref[...] = total[1]
    for copy in spares:
        copy.wait()


def add_kernel(a_ref, b_ref, out_ref):
    total = a_ref[...] + b_ref[...]
    if out_ref.shape == a_ref.shape:
        out_ref[...] = total
    else:
        for p in range(out_ref.shape[0]):
            out_ref[p] = total


def xor_exchange(x, bits, size, axis):
    return lax.ppermute(x, axis, [(i, i ^ bits) for i in range(size)])


def direct_kernel(slots, tiles_ref, own_ref, other_ref, out_ref, x_all, meta, sems):
    core = lax.axis_index("row") % 2
    edge = tiles_ref.shape[2]
    row_tiles = out_ref.shape[1] // edge
    at_meta = pl.ds(slots * edge, 8)
    count = tiles_ref.shape[0]
    metas = start_all([(tiles_ref.at[d, at_meta, :], meta.at[d]) for d in range(count)], sems)
    out_ref[...] = jnp.zeros_like(out_ref)
    x_all[0] = own_ref[...]
    x_all[1] = other_ref[...]
    for d in range(count):
        metas[d].wait()
        for k in range(slots):
            row, col, live = slot_of(slots, meta, d, k)
            lanes = pl.ds(pl.multiple_of((col % row_tiles) * edge, edge), edge)
            piece = col // row_tiles
            x = split(jnp.where(live, x_all[(piece % 2) ^ core, piece // 2, :, lanes], 0.0))
            u = split(tiles_ref[d, k * edge : (k + 1) * edge, :])
            here = pl.ds(pl.multiple_of(row * edge, edge), edge)
            out_ref[:, here] += tile_dot(x, u, NT)


def gather_sum_kernel(part_ref, direct_ref, out_ref):
    total = direct_ref[...]
    for r in range(part_ref.shape[0]):
        total = total + part_ref[r]
    for c in range(out_ref.shape[0]):
        out_ref[c] = total


def prep_kernel(order, w_ref, side_ref, wt_ref, side_t_ref, readout_ref, by_feature):
    wt = split(w_ref[...].T)
    wt_ref[0] = wt[0]
    wt_ref[1] = wt[1]
    me = lax.axis_index("col")
    block = w_ref.shape[0] // len(order)
    by_feature[...] = jnp.zeros_like(by_feature)
    for d, mask in enumerate(order):
        here = pl.ds(pl.multiple_of((me ^ mask) * block, block), block)
        by_feature[here, :8] = side_ref[d].T[:block, :]
    side_t_ref[...] = by_feature[:, :8]
    readout_ref[...] = by_feature[...].T[:8, :]


def ports_kernel(
    y_ref, wt_ref, side_t_ref, readout_ref, ports_ref, targets_ref, pred_ref, grad_ref, pre_p, hid_p
):
    me = lax.axis_index("col")
    cols, block, nodes = y_ref.shape
    feats = cols * block
    mine = pl.ds(pl.multiple_of(me * block, block), block)
    y = split(y_ref[...].reshape(feats, nodes))
    node = lax.broadcasted_iota(jnp.int32, (nodes, ports_ref.shape[1]), 0)
    pick = (node == ports_ref[...]).astype(BF16)
    yp = split(dot(y[0], pick, NN) + dot(y[1], pick, NN))
    pre_all = dot3((wt_ref[0], wt_ref[1]), yp, NN) + side_t_ref[:, 1:2]
    pre_p[...] = pre_all
    hid_all = pre_all * jax.nn.sigmoid(pre_all)
    hid_p[...] = hid_all
    outs = targets_ref.shape[0]
    pred = dot3(split(readout_ref[...]), split(hid_all), NN)[2 : 2 + outs]
    pred_ref[...] = pred
    err = pred - targets_ref[...]
    gow = dot3(split(err), split(hid_p[mine, :]), NT)
    pre_c = pre_p[mine, :]
    s = jax.nn.sigmoid(pre_c)
    port_grad = side_t_ref[mine, 2:3] * err[0:1, :] + side_t_ref[mine, 3:4] * err[1:2, :]
    grad_pre = port_grad * (s * (1.0 + pre_c * (1.0 - s)))
    gp = split(grad_pre)
    ones = jnp.ones((1, grad_pre.shape[1]), BF16)
    gb = dot(ones, gp[0], NT) + dot(ones, gp[1], NT)
    gw = dot3(gp, yp, NT)
    grad_ref[:block, :] = gw
    grad_ref[block:, :] = jnp.zeros((grad_ref.shape[0] - block, feats), F32)
    grad_ref[block : block + outs, :block] = gow
    grad_ref[block + outs : block + outs + 1, :block] = gb


def hidden_kernel(y_ref, wt_ref, side_t_ref, hidden_ref):
    me = lax.axis_index("col")
    cols, block, nodes = y_ref.shape
    mine = pl.ds(pl.multiple_of(me * block, block), block)
    y = split(y_ref[...].reshape(cols * block, nodes))
    pre = dot3((wt_ref[0, mine, :], wt_ref[1, mine, :]), y, NN) + side_t_ref[mine, 1:2]
    hidden_ref[...] = pre * jax.nn.sigmoid(pre)


def final_kernel(parts_ref, gw_ref, gb_ref, gow_ref):
    block = gw_ref.shape[0]
    outs = gow_ref.shape[0]
    total = parts_ref[0]
    for r in range(1, parts_ref.shape[0]):
        total = total + parts_ref[r]
    gw_ref[...] = total[:block, :]
    gow_ref[...] = total[block : block + outs, :block]
    gb_ref[...] = total[block + outs : block + outs + 1, :block]


def on_chip(x):
    return pltpu.with_memory_space_constraint(x, pltpu.VMEM)


def per_device(
    features,
    weight,
    layer_bias,
    out_weight,
    adj_tiles,
    tile_rows,
    tile_cols,
    tile_count,
    port_rows,
    targets,
):
    rows = lax.axis_size("row")
    cols = lax.axis_size("col")
    nodes, block = features.shape
    feats = weight.shape[0]
    slots, edge = adj_tiles.shape[2:4]
    outs = out_weight.shape[0]
    x_own = features.T
    half = (rows // 2, block, nodes)
    other_core = [(r, r ^ 1) for r in range(rows)]
    chips = [list(range(core, rows, 2)) for core in range(2)]
    base = slots * edge
    length = base + 8

    anywhere = pl.BlockSpec(memory_space=pl.ANY)
    packed, own_tiles = pl.pallas_call(
        functools.partial(pack_kernel, slots),
        in_specs=[SMEM, SMEM, SMEM, VMEM, VMEM, VMEM],
        out_specs=[VMEM, VMEM],
        out_shape=[jax.ShapeDtypeStruct((length, edge), F32), pltpu.VMEM((length, edge), F32)],
        name="pack",
    )(tile_rows, tile_cols, tile_count, adj_tiles.reshape(1, base, edge), layer_bias[None, :], out_weight)
    order = [0] + TILE_ORDER
    tiles = [own_tiles] + [xor_exchange(packed, d, cols, "col") for d in order[1:]]
    x_copies = jnp.broadcast_to(x_own[None], half)
    own_rows = lax.all_to_all(x_copies, "row", 0, 0, axis_index_groups=chips)
    other_rows = lax.ppermute(own_rows, "row", other_core)
    tiles = [on_chip(t) for t in tiles]

    meta = [pltpu.SMEM((cols, 8, edge), F32), pltpu.SemaphoreType.DMA((cols,))]
    keep, send, sides, spare_tiles = pl.pallas_call(
        functools.partial(mirror_kernel, slots, order),
        in_specs=[VMEM] * (cols + 1),
        out_specs=[VMEM] * 3 + [anywhere],
        out_shape=[
            pltpu.VMEM(half, F32),
            pltpu.VMEM(half, F32),
            pltpu.VMEM((cols, 8, edge), F32),
            jax.ShapeDtypeStruct((cols, length, edge), F32),
        ],
        scratch_shapes=[pltpu.VMEM((2,) + half, F32)] + meta + [pltpu.SemaphoreType.DMA((cols,))],
        name="mirror",
    )(*tiles, x_own)
    paired = pl.pallas_call(
        add_kernel,
        in_specs=[VMEM, VMEM],
        out_specs=VMEM,
        out_shape=pltpu.VMEM(half, F32),
        name="pair_sum",
    )(on_chip(keep), on_chip(lax.ppermute(send, "row", other_core)))
    parts = on_chip(lax.all_to_all(paired, "row", 0, 0, axis_index_groups=chips))
    direct = pl.pallas_call(
        functools.partial(direct_kernel, slots),
        in_specs=[VMEM] * 3,
        out_specs=VMEM,
        out_shape=pltpu.VMEM((block, nodes), F32),
        scratch_shapes=[pltpu.VMEM((2,) + half, F32)] + meta,
        name="direct",
    )(spare_tiles, on_chip(own_rows), on_chip(other_rows))
    wt, side_t, readout = pl.pallas_call(
        functools.partial(prep_kernel, order),
        in_specs=[VMEM] * 2,
        out_specs=[VMEM] * 3,
        out_shape=[
            pltpu.VMEM((2, feats, feats), BF16),
            pltpu.VMEM((feats, 8), F32),
            pltpu.VMEM((8, feats), F32),
        ],
        scratch_shapes=[pltpu.VMEM((feats, edge), F32)],
        name="prep",
    )(weight, on_chip(sides))
    wt, side_t, readout = on_chip(wt), on_chip(side_t), on_chip(readout)
    y_own = pl.pallas_call(
        gather_sum_kernel,
        in_specs=[VMEM, VMEM],
        out_specs=VMEM,
        out_shape=pltpu.VMEM((cols, block, nodes), F32),
        name="gather_sum",
    )(parts, on_chip(direct))
    y = on_chip(lax.all_to_all(y_own, "col", 0, 0))
    ports = port_rows.shape[1]
    predictions, grads = pl.pallas_call(
        ports_kernel,
        in_specs=[VMEM] * 6,
        out_specs=[VMEM, VMEM],
        out_shape=[
            jax.ShapeDtypeStruct((outs, ports), F32),
            pltpu.VMEM((block + 8, feats), F32),
        ],
        scratch_shapes=[pltpu.VMEM((feats, ports), F32)] * 2,
        name="ports",
    )(y, wt, side_t, readout, port_rows, targets)
    pair_grads = pl.pallas_call(
        add_kernel,
        in_specs=[VMEM, VMEM],
        out_specs=VMEM,
        out_shape=pltpu.VMEM((rows // 2, block + 8, feats), F32),
        name="pair_grads",
    )(on_chip(grads), on_chip(lax.ppermute(grads, "row", other_core)))
    all_grads = on_chip(lax.all_to_all(pair_grads, "row", 0, 0, axis_index_groups=chips))
    hidden_t = pl.pallas_call(
        hidden_kernel,
        in_specs=[VMEM] * 3,
        out_specs=VMEM,
        out_shape=jax.ShapeDtypeStruct((block, nodes), F32),
        name="hidden",
    )(y, wt, side_t)
    gw, gb, gow = pl.pallas_call(
        final_kernel,
        in_specs=[VMEM],
        out_specs=[VMEM] * 3,
        out_shape=[
            jax.ShapeDtypeStruct((block, feats), F32),
            jax.ShapeDtypeStruct((1, block), F32),
            jax.ShapeDtypeStruct((outs, block), F32),
        ],
        name="final",
    )(all_grads)
    return (hidden_t.T, predictions, gw.T, gb[0], gow)


def solution(mesh):
    placed = (
        P("row", "col"),
        P(),
        P("col"),
        P(None, "col"),
        P("row", "col", None, None, None),
        P("row", "col", None),
        P("row", "col", None),
        P("row", "col"),
        P("row", None),
        P(None, "row"),
    )
    return jax.shard_map(
        per_device,
        mesh=mesh,
        in_specs=placed,
        out_specs=(P("row", "col"), P(None, "row"), P(None, "col"), P("col"), P(None, "col")),
        check_vma=False,
    )
```

```python
import functools

import jax
import jax.numpy as jnp
from jax import lax
from jax.experimental import pallas as pl
from jax.experimental.pallas import tpu as pltpu
from jax.sharding import PartitionSpec as P

F32 = jnp.float32
BF16 = jnp.bfloat16
VMEM = pl.BlockSpec(memory_space=pltpu.VMEM)
SMEM = pl.BlockSpec(memory_space=pltpu.SMEM)
LIMIT = pltpu.CompilerParams(vmem_limit_bytes=16 * 2**20)
NN = (((1,), (0,)), ((), ()))
NT = (((1,), (1,)), ((), ()))
TILE_ORDER = [5, 1, 4, 7, 3, 2, 6]


def split(x):
    high = x.astype(BF16)
    low = (x - high.astype(F32)).astype(BF16)
    return high, low


def dot(a, b, dims):
    return lax.dot_general(a, b, dims, preferred_element_type=F32)


def dot3(a, b, dims):
    return dot(a[0], b[0], dims) + (dot(a[1], b[0], dims) + dot(a[0], b[1], dims))


def tile_dot(x, u, dims):
    rows = x[0].shape[0]
    wide = 1 if dims == NN else 0
    edge = u[0].shape[wide]
    every = dot(jnp.concatenate(x, axis=0), jnp.concatenate(u, axis=wide), dims)
    return every[:rows, :edge] + (every[rows:, :edge] + every[:rows, edge:] + every[rows:, edge:])


def pack_kernel(slots, rows_ref, cols_ref, count_ref, tiles_ref, bias_ref, readout_ref, out_ref, own_ref):
    edge = tiles_ref.shape[2]
    block = bias_ref.shape[1]
    outs = readout_ref.shape[0]
    base = slots * edge
    out_ref[:base, :] = tiles_ref[0]
    lane = lax.broadcasted_iota(jnp.int32, (1, edge), 1)
    meta = jnp.where(lane == 2 * slots, count_ref[0, 0], 0)
    for k in range(slots):
        meta = jnp.where(lane == k, rows_ref[0, 0, k], meta)
        meta = jnp.where(lane == slots + k, cols_ref[0, 0, k], meta)
    out_ref[base : base + 8, :] = jnp.zeros((8, edge), F32)
    out_ref[base : base + 1, :] = meta.astype(F32)
    out_ref[base + 1 : base + 2, :block] = bias_ref[...]
    out_ref[base + 2 : base + 2 + outs, :block] = readout_ref[...]
    own_ref[...] = out_ref[...]


def start_all(pairs, sems):
    copies = [pltpu.make_async_copy(src, dst, sems.at[i]) for i, (src, dst) in enumerate(pairs)]
    for copy in copies:
        copy.start()
    return copies


def slot_of(slots, meta, d, k):
    row, col, count = [meta[d, 0, at].astype(jnp.int32) for at in (k, slots + k, 2 * slots)]
    return row, col, k < count


def mirror_kernel(slots, order, *refs):
    tiles_refs, refs = refs[: len(order)], refs[len(order) :]
    x_hbm, keep_ref, send_ref, side_ref, copy_ref, total, x_ref, meta, meta_sems, copy_sems, x_sem, send_sem = refs
    x_copy = pltpu.make_async_copy(x_hbm, x_ref, x_sem)
    x_copy.start()
    edge = tiles_refs[0].shape[1]
    base = slots * edge
    row_tiles = x_ref.shape[1] // edge
    core = lax.axis_index("row") % 2
    metas = start_all([(ref.at[pl.ds(base, 8), :], meta.at[d]) for d, ref in enumerate(tiles_refs)], meta_sems)
    spares = start_all([(ref, copy_ref.at[d]) for d, ref in enumerate(tiles_refs)], copy_sems)
    total[...] = jnp.zeros_like(total)
    for d, ref in enumerate(tiles_refs):
        side_ref[d] = ref[base:, :]
    x_copy.wait()
    for d, ref in enumerate(tiles_refs):
        metas[d].wait()
        for k in range(slots):
            row, col, live = slot_of(slots, meta, d, k)
            x = x_ref[:, pl.ds(pl.multiple_of(row * edge, edge), edge)]
            x = split(jnp.where(live, x, 0.0))
            u = split(ref[k * edge : (k + 1) * edge, :])
            lanes = pl.ds(pl.multiple_of((col % row_tiles) * edge, edge), edge)
            piece = col // row_tiles
            total[(piece % 2) ^ core, piece // 2, :, lanes] += tile_dot(x, u, NN)
    sent = pltpu.make_async_copy(total.at[1], send_ref, send_sem)
    sent.start()
    keep_ref[...] = total[0]
    for copy in spares:
        copy.wait()
    sent.wait()


def add_kernel(a_ref, b_ref, out_ref):
    total = a_ref[...] + b_ref[...]
    if out_ref.shape == a_ref.shape:
        out_ref[...] = total
    else:
        for p in range(out_ref.shape[0]):
            out_ref[p] = total


def xor_exchange(x, bits, size, axis):
    return lax.ppermute(x, axis, [(i, i ^ bits) for i in range(size)])


def direct_kernel(slots, tiles_ref, own_ref, other_ref, out_ref, x_all, meta, sems):
    core = lax.axis_index("row") % 2
    edge = tiles_ref.shape[2]
    row_tiles = out_ref.shape[1] // edge
    at_meta = pl.ds(slots * edge, 8)
    count = tiles_ref.shape[0]
    metas = start_all([(tiles_ref.at[d, at_meta, :], meta.at[d]) for d in range(count)], sems)
    out_ref[...] = jnp.zeros_like(out_ref)
    x_all[0] = own_ref[...]
    x_all[1] = other_ref[...]
    for d in range(count):
        metas[d].wait()
        for k in range(slots):
            row, col, live = slot_of(slots, meta, d, k)
            lanes = pl.ds(pl.multiple_of((col % row_tiles) * edge, edge), edge)
            piece = col // row_tiles
            x = split(jnp.where(live, x_all[(piece % 2) ^ core, piece // 2, :, lanes], 0.0))
            u = split(tiles_ref[d, k * edge : (k + 1) * edge, :])
            here = pl.ds(pl.multiple_of(row * edge, edge), edge)
            out_ref[:, here] += tile_dot(x, u, NT)


def gather_sum_kernel(part_ref, direct_ref, out_ref):
    total = direct_ref[...]
    for r in range(part_ref.shape[0]):
        total = total + part_ref[r]
    for c in range(out_ref.shape[0]):
        out_ref[c] = total


def prep_kernel(order, w_ref, side_ref, wt_ref, side_t_ref, readout_ref, by_feature):
    wt = split(w_ref[...].T)
    wt_ref[0] = wt[0]
    wt_ref[1] = wt[1]
    me = lax.axis_index("col")
    block = w_ref.shape[0] // len(order)
    by_feature[...] = jnp.zeros_like(by_feature)
    for d, mask in enumerate(order):
        here = pl.ds(pl.multiple_of((me ^ mask) * block, block), block)
        by_feature[here, :8] = side_ref[d].T[:block, :]
    side_t_ref[...] = by_feature[:, :8]
    readout_ref[...] = by_feature[...].T[:8, :]


def ports_kernel(
    y_ref, wt_ref, side_t_ref, readout_ref, ports_ref, targets_ref, pred_ref, grad_ref, pre_p, hid_p
):
    me = lax.axis_index("col")
    cols, block, nodes = y_ref.shape
    feats = cols * block
    mine = pl.ds(pl.multiple_of(me * block, block), block)
    y = split(y_ref[...].reshape(feats, nodes))
    node = lax.broadcasted_iota(jnp.int32, (nodes, ports_ref.shape[1]), 0)
    pick = (node == ports_ref[...]).astype(BF16)
    yp = split(dot(y[0], pick, NN) + dot(y[1], pick, NN))
    pre_all = dot3((wt_ref[0], wt_ref[1]), yp, NN) + side_t_ref[:, 1:2]
    pre_p[...] = pre_all
    hid_all = pre_all * jax.nn.sigmoid(pre_all)
    hid_p[...] = hid_all
    outs = targets_ref.shape[0]
    pred = dot3(split(readout_ref[...]), split(hid_all), NN)[2 : 2 + outs]
    pred_ref[...] = pred
    err = pred - targets_ref[...]
    gow = dot3(split(err), split(hid_p[mine, :]), NT)
    pre_c = pre_p[mine, :]
    s = jax.nn.sigmoid(pre_c)
    port_grad = side_t_ref[mine, 2:3] * err[0:1, :] + side_t_ref[mine, 3:4] * err[1:2, :]
    grad_pre = port_grad * (s * (1.0 + pre_c * (1.0 - s)))
    gp = split(grad_pre)
    ones = jnp.ones((1, grad_pre.shape[1]), BF16)
    gb = dot(ones, gp[0], NT) + dot(ones, gp[1], NT)
    gw = dot3(gp, yp, NT)
    grad_ref[:block, :] = gw
    grad_ref[block:, :] = jnp.zeros((grad_ref.shape[0] - block, feats), F32)
    grad_ref[block : block + outs, :block] = gow
    grad_ref[block + outs : block + outs + 1, :block] = gb


def hidden_kernel(y_ref, wt_ref, side_t_ref, hidden_ref):
    me = lax.axis_index("col")
    cols, block, nodes = y_ref.shape
    mine = pl.ds(pl.multiple_of(me * block, block), block)
    y = split(y_ref[...].reshape(cols * block, nodes))
    pre = dot3((wt_ref[0, mine, :], wt_ref[1, mine, :]), y, NN) + side_t_ref[mine, 1:2]
    hidden_ref[...] = pre * jax.nn.sigmoid(pre)


def final_kernel(parts_ref, gw_ref, gb_ref, gow_ref):
    block = gw_ref.shape[0]
    outs = gow_ref.shape[0]
    total = parts_ref[0]
    for r in range(1, parts_ref.shape[0]):
        total = total + parts_ref[r]
    gw_ref[...] = total[:block, :]
    gow_ref[...] = total[block : block + outs, :block]
    gb_ref[...] = total[block + outs : block + outs + 1, :block]


def on_chip(x):
    return pltpu.with_memory_space_constraint(x, pltpu.VMEM)


def per_device(
    features,
    weight,
    layer_bias,
    out_weight,
    adj_tiles,
    tile_rows,
    tile_cols,
    tile_count,
    port_rows,
    targets,
):
    rows = lax.axis_size("row")
    cols = lax.axis_size("col")
    nodes, block = features.shape
    feats = weight.shape[0]
    slots, edge = adj_tiles.shape[2:4]
    outs = out_weight.shape[0]
    x_own = features.T
    half = (rows // 2, block, nodes)
    other_core = [(r, r ^ 1) for r in range(rows)]
    chips = [list(range(core, rows, 2)) for core in range(2)]
    base = slots * edge
    length = base + 8

    anywhere = pl.BlockSpec(memory_space=pl.ANY)
    packed, own_tiles = pl.pallas_call(
        functools.partial(pack_kernel, slots),
        in_specs=[SMEM, SMEM, SMEM, VMEM, VMEM, VMEM],
        out_specs=[VMEM, VMEM],
        out_shape=[jax.ShapeDtypeStruct((length, edge), F32), pltpu.VMEM((length, edge), F32)],
        name="pack",
    )(tile_rows, tile_cols, tile_count, adj_tiles.reshape(1, base, edge), layer_bias[None, :], out_weight)
    order = [0] + TILE_ORDER
    tiles = [own_tiles] + [xor_exchange(packed, d, cols, "col") for d in order[1:]]
    x_copies = jnp.broadcast_to(x_own[None], half)
    own_rows = lax.all_to_all(x_copies, "row", 0, 0, axis_index_groups=chips)
    other_rows = lax.ppermute(own_rows, "row", other_core)
    tiles = [on_chip(t) for t in tiles]

    meta = [pltpu.SMEM((cols, 8, edge), F32), pltpu.SemaphoreType.DMA((cols,))]
    keep, send, sides, spare_tiles = pl.pallas_call(
        functools.partial(mirror_kernel, slots, order),
        in_specs=[VMEM] * cols + [anywhere],
        out_specs=[VMEM, anywhere, VMEM, anywhere],
        out_shape=[
            pltpu.VMEM(half, F32),
            jax.ShapeDtypeStruct(half, F32),
            pltpu.VMEM((cols, 8, edge), F32),
            jax.ShapeDtypeStruct((cols, length, edge), F32),
        ],
        scratch_shapes=[pltpu.VMEM((2,) + half, F32), pltpu.VMEM((block, nodes), F32)]
        + meta
        + [pltpu.SemaphoreType.DMA((cols,))]
        + [pltpu.SemaphoreType.DMA] * 2,
        name="mirror",
    )(*tiles, x_own)
    paired = pl.pallas_call(
        add_kernel,
        in_specs=[VMEM, VMEM],
        out_specs=VMEM,
        out_shape=pltpu.VMEM(half, F32),
        name="pair_sum",
    )(on_chip(keep), on_chip(lax.ppermute(send, "row", other_core)))
    parts = on_chip(lax.all_to_all(paired, "row", 0, 0, axis_index_groups=chips))
    direct = pl.pallas_call(
        functools.partial(direct_kernel, slots),
        in_specs=[VMEM] * 3,
        out_specs=VMEM,
        out_shape=pltpu.VMEM((block, nodes), F32),
        scratch_shapes=[pltpu.VMEM((2,) + half, F32)] + meta,
        name="direct",
    )(spare_tiles, on_chip(own_rows), on_chip(other_rows))
    wt, side_t, readout = pl.pallas_call(
        functools.partial(prep_kernel, order),
        in_specs=[VMEM] * 2,
        out_specs=[VMEM] * 3,
        out_shape=[
            pltpu.VMEM((2, feats, feats), BF16),
            pltpu.VMEM((feats, 8), F32),
            pltpu.VMEM((8, feats), F32),
        ],
        scratch_shapes=[pltpu.VMEM((feats, edge), F32)],
        name="prep",
        compiler_params=LIMIT,
    )(weight, on_chip(sides))
    wt, side_t, readout = on_chip(wt), on_chip(side_t), on_chip(readout)
    y_own = pl.pallas_call(
        gather_sum_kernel,
        in_specs=[VMEM, VMEM],
        out_specs=VMEM,
        out_shape=pltpu.VMEM((cols, block, nodes), F32),
        name="gather_sum",
    )(parts, on_chip(direct))
    y = on_chip(lax.all_to_all(y_own, "col", 0, 0))
    ports = port_rows.shape[1]
    predictions, grads = pl.pallas_call(
        ports_kernel,
        in_specs=[VMEM] * 6,
        out_specs=[VMEM, VMEM],
        out_shape=[
            jax.ShapeDtypeStruct((outs, ports), F32),
            pltpu.VMEM((block + 8, feats), F32),
        ],
        scratch_shapes=[pltpu.VMEM((feats, ports), F32)] * 2,
        name="ports",
        compiler_params=LIMIT,
    )(y, wt, side_t, readout, port_rows, targets)
    pair_grads = pl.pallas_call(
        add_kernel,
        in_specs=[VMEM, VMEM],
        out_specs=VMEM,
        out_shape=pltpu.VMEM((rows // 2, block + 8, feats), F32),
        name="pair_grads",
    )(on_chip(grads), on_chip(lax.ppermute(grads, "row", other_core)))
    all_grads = on_chip(lax.all_to_all(pair_grads, "row", 0, 0, axis_index_groups=chips))
    hidden_t = pl.pallas_call(
        hidden_kernel,
        in_specs=[VMEM] * 3,
        out_specs=VMEM,
        out_shape=jax.ShapeDtypeStruct((block, nodes), F32),
        name="hidden",
        compiler_params=LIMIT,
    )(y, wt, side_t)
    gw, gb, gow = pl.pallas_call(
        final_kernel,
        in_specs=[VMEM],
        out_specs=[VMEM] * 3,
        out_shape=[
            jax.ShapeDtypeStruct((block, feats), F32),
            jax.ShapeDtypeStruct((1, block), F32),
            jax.ShapeDtypeStruct((outs, block), F32),
        ],
        name="final",
    )(all_grads)
    return (hidden_t.T, predictions, gw.T, gb[0], gow)


def solution(mesh):
    placed = (
        P("row", "col"),
        P(),
        P("col"),
        P(None, "col"),
        P("row", "col", None, None, None),
        P("row", "col", None),
        P("row", "col", None),
        P("row", "col"),
        P("row", None),
        P(None, "row"),
    )
    return jax.shard_map(
        per_device,
        mesh=mesh,
        in_specs=placed,
        out_specs=(P("row", "col"), P(None, "row"), P(None, "col"), P("col"), P(None, "col")),
        check_vma=False,
    )
```
